32 devices in a mesh: groups: 2 (over y), col: 16 (over z, x, core).
Axes of the slice: x: 2, y: 2, z: 4, core: 2. Of those that a mesh axis runs over, the one named last changes fastest.
Arguments:
- features: bfloat16 [16, 128, 768], P('groups', 'col'), parts along dimension 0, may hold values from -6 to 6
- column_table: bfloat16 [128, 768], P('col'), may hold values from -3 to 3
- dw_kernel: bfloat16 [7, 7, 768], replicated, may hold values from -0.875 to 0.875
- norm_gain: float32 [768], replicated, may hold values from 0.5 to 2
- expand_weight: bfloat16 [768, 3072], replicated, may hold values from -0.21875 to 0.21875
- reduce_weight: bfloat16 [3072, 768], replicated, may hold values from -0.109375 to 0.109375
- layer_scale: float32 [768], replicated, may hold values from 0.2 to 1
Outputs:
- disagreement: bfloat16 [16, 128, 768], P('groups', 'col'), parts along dimension 0
- grad_expand: float32 [1536, 3072], P(('groups', 'col')), parts along dimension 0
- grad_reduce: float32 [6144, 768], P(('groups', 'col')), parts along dimension 0
- grad_kernel: float32 [14, 7, 768], P('groups'), parts along dimension 0
- grad_gain: float32 [1536], P('groups'), parts along dimension 0
- grad_scale: float32 [1536], P('groups'), parts along dimension 0
The draws below stay inside these ranges and needn't reach their ends.
There are 2 independent parts, one for each index of `groups`. The reference program is written for one: setup_inputs(seed, part) draws one part's arguments, and reference() takes and returns one part's arrays. A program takes and returns all parts, laid end to end along the dimension named above; an argument that names none is the same for every part. Nothing has to cross between parts.
All inputs are finite; a program needn't handle non-finite values.
Results may differ from the reference program's by a relative error of at most 0.0096.
The reference program's roundings to bfloat16 on the way (of `normed`, `hidden`, `residual`, `dbranch` and `dpre`) count: a program that leaves them out, or rounds other values in their place, can miss the bound.
Values may be sent and summed in bfloat16 or wider, within the bound.
A program may use at most 128 MiB of HBM per device.

```python
import math
import jax
import jax.numpy as jnp
from jax import lax

C = 768
HID = 3072
ROWS = 8
WIDTH = 128


def with_spikes(drawn, rng, source, target, blocks, factor):
    def block_of(position):
        return (jnp.arange(drawn.shape[position]) // (drawn.shape[position] // blocks)).reshape((-1,) + (1,) * (drawn.ndim - 1 - position))

    near = jax.random.permutation(rng, blocks)[block_of(target)]
    far = (block_of(target) + blocks // 2) % blocks
    return jnp.where((block_of(source) == near) | (block_of(source) == far), factor * drawn, drawn)


def shard_levels(stream_key, extent, cuts, smallest, top_value):
    gain, own = 1.0, jax.random.fold_in(stream_key, 6)
    for dim, shards_of in cuts:
        draws = jnp.exp(jax.random.uniform(jax.random.fold_in(own, dim), (shards_of,), jnp.float32, smallest / len(cuts), top_value / len(cuts)))
        gain = gain * jnp.repeat(draws, extent[dim] // shards_of).reshape([-1 if axis == dim else 1 for axis in range(len(extent))])
    return gain


def noise(rng, extent, deviation, limit, shards=(), held_as=jnp.bfloat16):
    loudness = shard_levels(rng, extent, shards, -0.22, 0.18) if shards else 1.0
    values = jax.random.normal(rng, extent, jnp.float32) * deviation * loudness
    return jnp.minimum(jnp.maximum(values, -limit), limit).astype(held_as)


def noise_with(stream_key, extent, width, limit, shards, heavy, kind=jnp.bfloat16):
    values = width * jax.random.normal(stream_key, extent, jnp.float32)
    if shards:
        values = values * shard_levels(stream_key, extent, shards, -0.22, 0.18)
    return jnp.clip(with_spikes(values, jax.random.fold_in(stream_key, 3), *heavy), -limit, limit).astype(kind)


def setup_inputs(seed: int = 0, part: int = 0) -> dict:
    splits = jax.random.split(jax.random.key(seed), 8)
    part_keys = jax.random.split(jax.random.fold_in(splits[7], part), 8)
    return {
        "features": noise_with(part_keys[0], (ROWS, WIDTH, C), 1.0, 6.0, ((1, 16),), (1, 2, 16, 2.0)),
        "column_table": noise(splits[1], (WIDTH, C), 0.5, 3.0, ((0, 16),)),
        "dw_kernel": noise(splits[2], (7, 7, C), 49 ** -0.5, 0.875),
        "norm_gain": jnp.clip(jnp.exp(jax.random.uniform(splits[3], (C,), jnp.float32, math.log(0.5), math.log(2.0))), 0.5, 2.0),
        "expand_weight": noise(splits[4], (C, HID), C ** -0.5, 0.21875),
        "reduce_weight": noise(splits[5], (HID, C), HID ** -0.5, 0.109375),
        "layer_scale": jnp.clip(jnp.exp(jax.random.uniform(splits[6], (C,), jnp.float32, math.log(0.2), math.log(1.0))), 0.2, 1.0),
    }


def gelu_parts(pre):
    normal_cdf = 0.5 * (1.0 + jax.scipy.special.erf(pre * 0.7071067811865476))
    density = jnp.exp(-0.5 * pre * pre) * 0.3989422804014327
    return (pre * normal_cdf, normal_cdf + pre * density)

def forward(view, kernel_f, norm_gain, expand_weight, reduce_weight, layer_scale):
    row_count, col_count, channels = view.shape
    padded = jnp.pad(view.astype(jnp.float32), ((3, 3), (3, 3), (0, 0)))
    conv = jnp.zeros((row_count, col_count, channels), jnp.float32)
    for row_off in range(7):
        for col_off in range(7):
            conv = conv + kernel_f[row_off, col_off] * padded[row_off:row_off + row_count, col_off:col_off + col_count]
    mean_val = lax.optimization_barrier(jnp.mean(conv, axis=-1, keepdims=True))
    centred = conv - mean_val
    variance = lax.optimization_barrier(jnp.mean(centred * centred, axis=-1, keepdims=True))
    inverse = lax.rsqrt(variance + 1e-06)
    nhat = centred * inverse
    normed = (nhat * norm_gain).astype(jnp.bfloat16).reshape(-1, channels)
    pre = jnp.dot(normed, expand_weight, preferred_element_type=jnp.float32)
    activated, gelu_slope = gelu_parts(pre)
    hidden = activated.astype(jnp.bfloat16)
    branch = jnp.dot(hidden, reduce_weight, preferred_element_type=jnp.float32)
    output = (view.astype(jnp.float32) + layer_scale * branch.reshape(view.shape)).astype(jnp.bfloat16)
    return (output, (padded, nhat, inverse, normed, gelu_slope, hidden, branch))

def backward(out_grad, saved, norm_gain, expand_weight, reduce_weight, layer_scale):
    padded, nhat, inverse, normed, gelu_slope, hidden, branch = saved
    row_count, col_count, channels = out_grad.shape
    flat_grad = out_grad.reshape(-1, channels)
    grad_scale = lax.optimization_barrier(jnp.sum(branch * flat_grad, axis=0))
    dbranch = (layer_scale * flat_grad).astype(jnp.bfloat16)
    grad_reduce = jnp.dot(hidden.T, dbranch, preferred_element_type=jnp.float32)
    dhidden = jnp.dot(dbranch, reduce_weight.T, preferred_element_type=jnp.float32)
    dpre = (dhidden * gelu_slope).astype(jnp.bfloat16)
    grad_expand = jnp.dot(normed.T, dpre, preferred_element_type=jnp.float32)
    dnormed = jnp.dot(dpre, expand_weight.T, preferred_element_type=jnp.float32).reshape(out_grad.shape)
    grad_gain = lax.optimization_barrier(jnp.sum(dnormed * nhat, axis=(0, 1)))
    scaled = dnormed * norm_gain
    dconv = inverse * (scaled - lax.optimization_barrier(jnp.mean(scaled, axis=-1, keepdims=True)) - nhat * lax.optimization_barrier(jnp.mean(scaled * nhat, axis=-1, keepdims=True)))
    kernel_rows = []
    for row_off in range(7):
        kernel_cols = []
        for col_off in range(7):
            window = padded[row_off:row_off + row_count, col_off:col_off + col_count]
            kernel_cols.append(lax.optimization_barrier(jnp.sum(window * dconv, axis=(0, 1))))
        kernel_rows.append(jnp.stack(kernel_cols))
    grad_kernel = jnp.stack(kernel_rows)
    return (grad_expand, grad_reduce, grad_kernel, grad_gain, grad_scale)

def reference(features, column_table, dw_kernel, norm_gain, expand_weight, reduce_weight, layer_scale):
    table_f = column_table.astype(jnp.float32)
    view_a = (features.astype(jnp.float32) + table_f).astype(jnp.bfloat16)
    view_b = (features[:, ::-1].astype(jnp.float32) + table_f).astype(jnp.bfloat16)
    kernel_f = dw_kernel.astype(jnp.float32)
    out_a, saved_a = forward(view_a, kernel_f, norm_gain, expand_weight, reduce_weight, layer_scale)
    out_b, saved_b = forward(view_b, kernel_f, norm_gain, expand_weight, reduce_weight, layer_scale)
    difference = out_a.astype(jnp.float32) - out_b[:, ::-1].astype(jnp.float32)
    disagreement = difference.astype(jnp.bfloat16)
    residual = (difference * (1.0 / math.sqrt(ROWS * WIDTH))).astype(jnp.bfloat16)
    residual = lax.optimization_barrier(residual)
    grad_a = residual.astype(jnp.float32)
    grad_b = -residual[:, ::-1].astype(jnp.float32)
    parts_a = backward(grad_a, saved_a, norm_gain, expand_weight, reduce_weight, layer_scale)
    parts_b = backward(grad_b, saved_b, norm_gain, expand_weight, reduce_weight, layer_scale)
    return (disagreement, parts_a[0] + parts_b[0], parts_a[1] + parts_b[1], parts_a[2] + parts_b[2], parts_a[3] + parts_b[3], parts_a[4] + parts_b[4])
```

```python
import math

import jax
import jax.numpy as jnp
from jax import lax
from jax.sharding import PartitionSpec as P


def permuted(block, target):
    count = lax.axis_size("col")
    return lax.ppermute(block, "col", [(i, target(i)) for i in range(count)])


def gelu_parts(pre):
    normal_cdf = 0.5 * (1.0 + jax.scipy.special.erf(pre * 0.7071067811865476))
    density = jnp.exp(-0.5 * pre * pre) * 0.3989422804014327
    return (pre * normal_cdf, normal_cdf + pre * density)


def with_halo(block, width):
    count = lax.axis_size("col")
    forward = [(i, i + 1) for i in range(count - 1)]
    backward = [(target, source) for source, target in forward]
    low = lax.ppermute(block[:, :, -width:], "col", forward)
    high = lax.ppermute(block[:, :, :width], "col", backward)
    return jnp.concatenate([low, block, high], axis=2)


def pick(array, index, axis):
    return lax.dynamic_index_in_dim(array, index, axis, keepdims=False)


def outer_scatter(partial):
    outer = partial.shape[0]
    count = lax.axis_size("col")
    mine = lax.axis_index("col") // 4
    rounded = partial.astype(jnp.bfloat16)
    total = pick(partial, mine, 0)
    for step in range(1, outer):
        block = pick(rounded, lax.rem(mine + step, outer), 0)
        got = permuted(block, lambda i: (i + 4 * step) % count)
        total = total + got.astype(jnp.float32)
    return total


def all_sum(block):
    count = lax.axis_size("col")
    for bit in range(count.bit_length() - 1):
        block = block + permuted(block, lambda i: i ^ (1 << bit))
    return block


def on_device(
    features, column_table, dw_kernel, norm_gain, expand_weight, reduce_weight, layer_scale
):
    row_count, col_count, channels = features.shape
    count = lax.axis_size("col")
    outer = count // 4
    me = lax.axis_index("col")
    core = lax.rem(me, 2)
    side = lax.rem(me // 2, 2)
    total_cols = col_count * count
    hidden_size = expand_weight.shape[1]
    pixels = row_count * col_count

    mirrored_table = permuted(column_table, lambda i: count - 1 - i)[::-1]
    tables = jnp.stack([column_table, mirrored_table]).astype(jnp.float32)
    views = (features.astype(jnp.float32)[None] + tables[:, None]).astype(jnp.bfloat16)
    kernel_f = dw_kernel.astype(jnp.float32)
    kernels = jnp.stack([kernel_f, kernel_f[:, ::-1]])
    widened = with_halo(views, 3)
    padded = jnp.pad(widened.astype(jnp.float32), ((0, 0), (3, 3), (0, 0), (0, 0)))
    conv = jnp.zeros((2, row_count, col_count, channels), jnp.float32)
    for row_off in range(7):
        for col_off in range(7):
            weights_here = kernels[:, row_off, col_off][:, None, None, :]
            conv = (
                conv
                + weights_here
                * padded[:, row_off : row_off + row_count, col_off : col_off + col_count]
            )
    mean_val = jnp.mean(conv, axis=-1, keepdims=True)
    centred = conv - mean_val
    variance = jnp.mean(centred * centred, axis=-1, keepdims=True)
    inverse = lax.rsqrt(variance + 1e-06)
    nhat = centred * inverse
    normed = (nhat * norm_gain).astype(jnp.bfloat16).reshape(-1, channels)
    pre = jnp.dot(normed, expand_weight, preferred_element_type=jnp.float32)
    activated, gelu_slope = gelu_parts(pre)
    hidden = activated.astype(jnp.bfloat16)
    branch = jnp.dot(hidden, reduce_weight, preferred_element_type=jnp.float32)
    outputs = (views.astype(jnp.float32) + layer_scale * branch.reshape(conv.shape)).astype(
        jnp.bfloat16
    )
    difference = outputs[0].astype(jnp.float32) - outputs[1].astype(jnp.float32)
    disagreement = difference.astype(jnp.bfloat16)
    residual = (difference * (1.0 / math.sqrt(row_count * total_cols))).astype(jnp.bfloat16)
    residual = lax.optimization_barrier(residual)
    flat_grad = residual.astype(jnp.float32).reshape(pixels, channels)
    branches = branch.reshape(2, pixels, channels)
    grad_scale_local = jnp.sum((branches[0] - branches[1]) * flat_grad, axis=0)
    dbranch = (layer_scale * flat_grad).astype(jnp.bfloat16)

    hiddens = hidden.astype(jnp.float32).reshape(2, pixels, hidden_size)
    contrast = (hiddens[0] - hiddens[1]).astype(jnp.bfloat16)
    contrast_t = contrast.T.reshape(outer, 2, 2, hidden_size // count, pixels)
    other_core = lambda i: i ^ 1
    other_side = lambda i: i ^ 2
    contrast_pair = jnp.concatenate(
        [pick(contrast_t, core, 2), permuted(pick(contrast_t, 1 - core, 2), other_core)], axis=-1
    )
    dbranch_pair = jnp.concatenate([dbranch, permuted(dbranch, other_core)], axis=0)
    contrast_quad = jnp.concatenate(
        [pick(contrast_pair, side, 1), permuted(pick(contrast_pair, 1 - side, 1), other_side)],
        axis=-1,
    )
    dbranch_quad = jnp.concatenate([dbranch_pair, permuted(dbranch_pair, other_side)], axis=0)
    reduce_quad = jnp.dot(
        contrast_quad.reshape(-1, 4 * pixels), dbranch_quad, preferred_element_type=jnp.float32
    ).reshape(outer, hidden_size // count, channels)
    grad_reduce = outer_scatter(reduce_quad)

    dhidden = lax.dot_general(
        dbranch, reduce_weight, (((1,), (1,)), ((), ())), preferred_element_type=jnp.float32
    )
    slopes = gelu_slope.reshape(2, pixels, hidden_size)
    dpre = jnp.stack([dhidden * slopes[0], -dhidden * slopes[1]]).astype(jnp.bfloat16)
    dpre = dpre.reshape(2 * pixels, hidden_size)

    normed_t = normed.T.reshape(outer, 2, 2, channels // count, 2 * pixels)
    normed_pair = jnp.concatenate(
        [pick(normed_t, core, 2), permuted(pick(normed_t, 1 - core, 2), other_core)], axis=-1
    )
    dpre_pair = jnp.concatenate([dpre, permuted(dpre, other_core)], axis=0)

    def expand_part(which):
        rows = pick(normed_pair, which, 1).reshape(-1, 4 * pixels)
        return jnp.dot(rows, dpre_pair, preferred_element_type=jnp.float32)

    sent = permuted(expand_part(1 - side).astype(jnp.bfloat16), other_side)
    expand_quad = expand_part(side) + sent.astype(jnp.float32)
    grad_expand = outer_scatter(expand_quad.reshape(outer, channels // count, hidden_size))

    dnormed = lax.dot_general(
        dpre, expand_weight, (((1,), (1,)), ((), ())), preferred_element_type=jnp.float32
    ).reshape(conv.shape)
    grad_gain_local = jnp.sum(dnormed * nhat, axis=(0, 1, 2))
    scaled = dnormed * norm_gain
    dconv = inverse * (
        scaled
        - jnp.mean(scaled, axis=-1, keepdims=True)
        - nhat * jnp.mean(scaled * nhat, axis=-1, keepdims=True)
    )
    kernel_rows = []
    for row_off in range(7):
        kernel_cols = []
        for col_off in range(7):
            window = padded[:, row_off : row_off + row_count, col_off : col_off + col_count]
            kernel_cols.append(jnp.sum(window * dconv, axis=(1, 2)))
        kernel_rows.append(jnp.stack(kernel_cols, axis=1))
    view_kernels = jnp.stack(kernel_rows, axis=1)
    kernel_local = view_kernels[0] + view_kernels[1][:, ::-1]
    small = jnp.concatenate(
        [kernel_local.reshape(49, channels), grad_gain_local[None], grad_scale_local[None]], axis=0
    )
    small = all_sum(small)
    return (
        disagreement,
        grad_expand,
        grad_reduce,
        small[:49].reshape(7, 7, channels),
        small[49],
        small[50],
    )


def solution(mesh):
    in_specs = (P("groups", "col", None), P("col", None), P(), P(), P(), P(), P())
    out_specs = (
        P("groups", "col", None),
        P(("groups", "col"), None),
        P(("groups", "col"), None),
        P("groups", None, None),
        P("groups"),
        P("groups"),
    )
    return jax.shard_map(
        on_device, mesh=mesh, in_specs=in_specs, out_specs=out_specs, check_vma=False
    )
```

```python
import math

import jax
import jax.numpy as jnp
from jax import lax
from jax.experimental import pallas as pl
from jax.experimental.pallas import tpu as pltpu
from jax.sharding import PartitionSpec as P


def permuted(block, target):
    count = lax.axis_size("col")
    return lax.ppermute(block, "col", [(i, target(i)) for i in range(count)])


def gelu_parts(pre):
    normal_cdf = 0.5 * (1.0 + jax.scipy.special.erf(pre * 0.7071067811865476))
    density = jnp.exp(-0.5 * pre * pre) * 0.3989422804014327
    return (pre * normal_cdf, normal_cdf + pre * density)


def with_halo(block, width):
    count = lax.axis_size("col")
    forward = [(i, i + 1) for i in range(count - 1)]
    backward = [(target, source) for source, target in forward]
    low = lax.ppermute(block[:, :, -width:], "col", forward)
    high = lax.ppermute(block[:, :, :width], "col", backward)
    return jnp.concatenate([low, block, high], axis=2)


def pick(array, index, axis):
    return lax.dynamic_index_in_dim(array, index, axis, keepdims=False)


def outer_exchange(rounded):
    outer = rounded.shape[0]
    count = lax.axis_size("col")
    mine = lax.axis_index("col") // 4
    return [
        permuted(pick(rounded, lax.rem(mine + step, outer), 0), lambda i: (i + 4 * step) % count)
        for step in range(1, outer)
    ]


def outer_total(partial, arrived):
    total = pick(partial, lax.axis_index("col") // 4, 0)
    for block in arrived:
        total = total + block.astype(jnp.float32)
    return total


def tail_kernel(
    dpre_ref, weight_ref, nhat_ref, inverse_ref, gain_ref, scale_ref, views_ref, out_ref, dconv_ref
):
    _, rows, wide, channels = views_ref.shape
    cols = wide - 6
    dnormed = lax.dot_general(
        dpre_ref[...],
        weight_ref[...],
        (((1,), (1,)), ((), ())),
        preferred_element_type=jnp.float32,
    )
    nhat = nhat_ref[...]
    out_ref[49:50] = jnp.sum(dnormed * nhat, axis=0, keepdims=True)
    out_ref[50:51] = scale_ref[...]
    scaled = dnormed * gain_ref[...]
    dconv = inverse_ref[...] * (
        scaled
        - jnp.mean(scaled, axis=-1, keepdims=True)
        - nhat * jnp.mean(scaled * nhat, axis=-1, keepdims=True)
    )
    dconv_ref[...] = dconv.reshape(dconv_ref.shape)

    def channel_tile(tile, carry):
        lanes = pl.ds(pl.multiple_of(tile * 128, 128), 128)
        sums = [[jnp.zeros((cols, 128), jnp.float32) for _ in range(7)] for _ in range(7)]
        for view in range(2):
            grads = [dconv_ref[view, row, :, lanes] for row in range(rows)]
            for source in range(rows):
                for col_off in range(7):
                    window = views_ref[view, source, col_off : col_off + cols, lanes]
                    place = col_off if view == 0 else 6 - col_off
                    for row_off in range(7):
                        row = source - row_off + 3
                        if 0 <= row < rows:
                            sums[row_off][place] = sums[row_off][place] + window * grads[row]
        for row_off in range(7):
            for col_off in range(7):
                index = row_off * 7 + col_off
                out_ref[index : index + 1, lanes] = jnp.sum(
                    sums[row_off][col_off], axis=0, keepdims=True
                )
        return carry

    lax.fori_loop(0, channels // 128, channel_tile, 0)


def tail(dpre, expand_weight, nhat, inverse, norm_gain, grad_scale, widened):
    channels = nhat.shape[-1]
    view_count, rows, wide, _ = widened.shape
    return pl.pallas_call(
        tail_kernel,
        out_shape=jax.ShapeDtypeStruct((51, channels), jnp.float32),
        scratch_shapes=[pltpu.VMEM((view_count, rows, wide - 6, channels), jnp.float32)],
        compiler_params=pltpu.CompilerParams(vmem_limit_bytes=32 << 20),
        cost_estimate=pl.CostEstimate(
            flops=20_000_000_000, bytes_accessed=30_000_000, transcendentals=0
        ),
    )(
        dpre,
        expand_weight,
        nhat.reshape(-1, channels),
        inverse.reshape(-1, 1),
        norm_gain[None],
        grad_scale[None],
        widened.astype(jnp.float32),
    )


def after(value, *others):
    return lax.optimization_barrier((value, *others))[0]


def all_sum(block):
    count = lax.axis_size("col")
    for bit in range(count.bit_length() - 1):
        block = block + permuted(block, lambda i: i ^ (1 << bit))
    return block


def on_device(
    features, column_table, dw_kernel, norm_gain, expand_weight, reduce_weight, layer_scale
):
    row_count, col_count, channels = features.shape
    count = lax.axis_size("col")
    outer = count // 4
    me = lax.axis_index("col")
    core = lax.rem(me, 2)
    side = lax.rem(me // 2, 2)
    total_cols = col_count * count
    hidden_size = expand_weight.shape[1]
    pixels = row_count * col_count

    mirrored_table = permuted(column_table, lambda i: count - 1 - i)[::-1]
    tables = jnp.stack([column_table, mirrored_table]).astype(jnp.float32)
    views = (features.astype(jnp.float32)[None] + tables[:, None]).astype(jnp.bfloat16)
    kernel_f = dw_kernel.astype(jnp.float32)
    kernels = jnp.stack([kernel_f, kernel_f[:, ::-1]])
    widened = with_halo(views, 3)
    padded = jnp.pad(widened.astype(jnp.float32), ((0, 0), (3, 3), (0, 0), (0, 0)))
    conv = jnp.zeros((2, row_count, col_count, channels), jnp.float32)
    for row_off in range(7):
        for col_off in range(7):
            weights_here = kernels[:, row_off, col_off][:, None, None, :]
            conv = (
                conv
                + weights_here
                * padded[:, row_off : row_off + row_count, col_off : col_off + col_count]
            )
    mean_val = jnp.mean(conv, axis=-1, keepdims=True)
    centred = conv - mean_val
    variance = jnp.mean(centred * centred, axis=-1, keepdims=True)
    inverse = lax.rsqrt(variance + 1e-06)
    nhat = centred * inverse
    normed = (nhat * norm_gain).astype(jnp.bfloat16).reshape(-1, channels)
    pre = jnp.dot(normed, expand_weight, preferred_element_type=jnp.float32)
    activated, gelu_slope = gelu_parts(pre)
    hidden = lax.reduce_precision(activated, 8, 7).astype(jnp.bfloat16)
    branch = jnp.dot(hidden, reduce_weight, preferred_element_type=jnp.float32)
    outputs = (views.astype(jnp.float32) + layer_scale * branch.reshape(conv.shape)).astype(
        jnp.bfloat16
    )
    difference = outputs[0].astype(jnp.float32) - outputs[1].astype(jnp.float32)
    disagreement = difference.astype(jnp.bfloat16)
    residual = (difference * (1.0 / math.sqrt(row_count * total_cols))).astype(jnp.bfloat16)
    residual = lax.optimization_barrier(residual)
    flat_grad = residual.astype(jnp.float32).reshape(pixels, channels)
    branches = branch.reshape(2, pixels, channels)
    grad_scale_local = jnp.sum((branches[0] - branches[1]) * flat_grad, axis=0)
    dbranch = (layer_scale * flat_grad).astype(jnp.bfloat16)

    hiddens = hidden.astype(jnp.float32).reshape(2, pixels, hidden_size)
    contrast = (hiddens[0] - hiddens[1]).astype(jnp.bfloat16)
    contrast_t = contrast.T.reshape(outer, 2, 2, hidden_size // count, pixels)
    other_core = lambda i: i ^ 1
    other_side = lambda i: i ^ 2
    contrast_pair = jnp.concatenate(
        [pick(contrast_t, core, 2), permuted(pick(contrast_t, 1 - core, 2), other_core)], axis=-1
    )
    dbranch_pair = jnp.concatenate([dbranch, permuted(dbranch, other_core)], axis=0)
    contrast_quad = jnp.concatenate(
        [pick(contrast_pair, side, 1), permuted(pick(contrast_pair, 1 - side, 1), other_side)],
        axis=-1,
    )
    dbranch_quad = jnp.concatenate([dbranch_pair, permuted(dbranch_pair, other_side)], axis=0)
    reduce_quad = jnp.dot(
        contrast_quad.reshape(-1, 4 * pixels), dbranch_quad, preferred_element_type=jnp.float32
    ).reshape(outer, hidden_size // count, channels)
    dhidden = lax.dot_general(
        dbranch, reduce_weight, (((1,), (1,)), ((), ())), preferred_element_type=jnp.float32
    )
    slopes = gelu_slope.reshape(2, pixels, hidden_size)
    dpre = jnp.stack([dhidden * slopes[0], -dhidden * slopes[1]]).astype(jnp.bfloat16)
    dpre = dpre.reshape(2 * pixels, hidden_size)

    normed_t = normed.T.reshape(outer, 2, 2, channels // count, 2 * pixels)
    normed_pair = jnp.concatenate(
        [pick(normed_t, core, 2), permuted(pick(normed_t, 1 - core, 2), other_core)], axis=-1
    )
    dpre_pair = jnp.concatenate([dpre, permuted(dpre, other_core)], axis=0)

    def expand_part(which):
        rows = pick(normed_pair, which, 1).reshape(-1, 4 * pixels)
        return jnp.dot(rows, dpre_pair, preferred_element_type=jnp.float32)

    leaving = expand_part(1 - side).astype(jnp.bfloat16)
    arrived = permuted(leaving, other_side)
    reduce_rounded = reduce_quad.astype(jnp.bfloat16)
    reduce_arrived = outer_exchange(reduce_rounded)
    small = tail(
        after(dpre, leaving, reduce_rounded),
        expand_weight,
        nhat,
        inverse,
        norm_gain,
        grad_scale_local,
        widened,
    )
    arrived, small, *reduce_arrived = lax.optimization_barrier((arrived, small, *reduce_arrived))
    expand_quad = expand_part(side) + arrived.astype(jnp.float32)
    expand_quad = expand_quad.reshape(outer, channels // count, hidden_size)
    expand_arrived = outer_exchange(expand_quad.astype(jnp.bfloat16))
    grad_reduce = outer_total(reduce_quad, reduce_arrived)
    small = all_sum(small)
    grad_expand = outer_total(expand_quad, expand_arrived)
    return (
        disagreement,
        grad_expand,
        grad_reduce,
        small[:49].reshape(7, 7, channels),
        small[49],
        small[50],
    )


def solution(mesh):
    in_specs = (P("groups", "col", None), P("col", None), P(), P(), P(), P(), P())
    out_specs = (
        P("groups", "col", None),
        P(("groups", "col"), None),
        P(("groups", "col"), None),
        P("groups", None, None),
        P("groups"),
        P("groups"),
    )
    return jax.shard_map(
        on_device, mesh=mesh, in_specs=in_specs, out_specs=out_specs, check_vma=False
    )
```

```python
import math

import jax
import jax.numpy as jnp
from jax import lax
from jax.experimental import pallas as pl
from jax.experimental.pallas import tpu as pltpu
from jax.sharding import PartitionSpec as P


def permuted(block, target):
    count = lax.axis_size("col")
    return lax.ppermute(block, "col", [(i, target(i)) for i in range(count)])


def gelu_parts(pre):
    normal_cdf = 0.5 * (1.0 + jax.scipy.special.erf(pre * 0.7071067811865476))
    density = jnp.exp(-0.5 * pre * pre) * 0.3989422804014327
    return (pre * normal_cdf, normal_cdf + pre * density)


def shifted(block, step):
    count = lax.axis_size("col")
    return lax.ppermute(
        block, "col", [(i, i + step) for i in range(count) if 0 <= i + step < count]
    )


def reflected(block, last):
    count = lax.axis_size("col")
    return lax.ppermute(
        block, "col", [(i, last - i) for i in range(count) if 0 <= last - i < count]
    )


def rounded_f32(value):
    return lax.reduce_precision(value, 8, 7)


def pick(array, index, axis):
    return lax.dynamic_index_in_dim(array, index, axis, keepdims=False)


def outer_exchange(rounded):
    outer = rounded.shape[0]
    count = lax.axis_size("col")
    mine = lax.axis_index("col") // 4
    return [
        permuted(pick(rounded, lax.rem(mine + step, outer), 0), lambda i: (i + 4 * step) % count)
        for step in range(1, outer)
    ]


def outer_total(partial, arrived):
    total = pick(partial, lax.axis_index("col") // 4, 0)
    for block in arrived:
        total = total + block.astype(jnp.float32)
    return total


def tail_kernel(
    dpre_ref, weight_ref, nhat_ref, inverse_ref, gain_ref, scale_ref, views_ref, out_ref, dconv_ref
):
    _, rows, wide, channels = views_ref.shape
    cols = wide - 6
    dnormed = lax.dot_general(
        dpre_ref[...],
        weight_ref[...],
        (((1,), (1,)), ((), ())),
        preferred_element_type=jnp.float32,
    )
    nhat = nhat_ref[...]
    out_ref[49:50] = jnp.sum(dnormed * nhat, axis=0, keepdims=True)
    out_ref[50:51] = scale_ref[...]
    out_ref[51:64] = jnp.zeros((13, channels), jnp.float32)
    scaled = dnormed * gain_ref[...]
    dconv = inverse_ref[...] * (
        scaled
        - jnp.mean(scaled, axis=-1, keepdims=True)
        - nhat * jnp.mean(scaled * nhat, axis=-1, keepdims=True)
    )
    dconv_ref[...] = dconv.reshape(dconv_ref.shape)

    def channel_tile(tile, carry):
        lanes = pl.ds(pl.multiple_of(tile * 128, 128), 128)
        sums = [[jnp.zeros((cols, 128), jnp.float32) for _ in range(7)] for _ in range(7)]
        for view in range(2):
            grads = [dconv_ref[view, row, :, lanes] for row in range(rows)]
            for source in range(rows):
                for col_off in range(7):
                    window = views_ref[view, source, col_off : col_off + cols, lanes]
                    place = col_off if view == 0 else 6 - col_off
                    for row_off in range(7):
                        row = source - row_off + 3
                        if 0 <= row < rows:
                            sums[row_off][place] = sums[row_off][place] + window * grads[row]
        for row_off in range(7):
            for col_off in range(7):
                index = row_off * 7 + col_off
                out_ref[index : index + 1, lanes] = jnp.sum(
                    sums[row_off][col_off], axis=0, keepdims=True
                )
        return carry

    lax.fori_loop(0, channels // 128, channel_tile, 0)


def tail(dpre, expand_weight, nhat, inverse, norm_gain, grad_scale, widened):
    channels = nhat.shape[-1]
    view_count, rows, wide, _ = widened.shape
    return pl.pallas_call(
        tail_kernel,
        out_shape=jax.ShapeDtypeStruct((64, channels), jnp.float32),
        scratch_shapes=[pltpu.VMEM((view_count, rows, wide - 6, channels), jnp.float32)],
        compiler_params=pltpu.CompilerParams(vmem_limit_bytes=32 << 20),
        cost_estimate=pl.CostEstimate(
            flops=20_000_000_000, bytes_accessed=30_000_000, transcendentals=0
        ),
    )(
        dpre,
        expand_weight,
        nhat.reshape(-1, channels),
        inverse.reshape(-1, 1),
        norm_gain[None],
        grad_scale[None],
        widened,
    )


def after(value, *others):
    return lax.optimization_barrier((value, *others))[0]


def on_device(
    features, column_table, dw_kernel, norm_gain, expand_weight, reduce_weight, layer_scale
):
    row_count, col_count, channels = features.shape
    count = lax.axis_size("col")
    outer = count // 4
    me = lax.axis_index("col")
    core = lax.rem(me, 2)
    side = lax.rem(me // 2, 2)
    total_cols = col_count * count
    hidden_size = expand_weight.shape[1]
    pixels = row_count * col_count

    edge = jnp.concatenate([features, column_table[None]], axis=0)
    low = shifted(edge[:, -3:], 1)
    high = shifted(edge[:, :3], -1)
    mirror = reflected(column_table, count - 1)
    mirror_low = reflected(column_table[:3], count)
    mirror_high = reflected(column_table[-3:], count - 2)
    wide = jnp.concatenate([low, edge, high], axis=1).astype(jnp.float32)
    mirror_wide = jnp.concatenate([mirror_high, mirror, mirror_low], axis=0).astype(jnp.float32)
    mirror_wide = jnp.concatenate(
        [mirror_wide[i : i + 1] for i in reversed(range(col_count + 6))], axis=0
    )
    tables = jnp.stack([wide[-1], mirror_wide])
    widened = rounded_f32(wide[None, :-1] + tables[:, None])
    views = widened[:, :, 3:-3]
    kernel_f = dw_kernel.astype(jnp.float32)
    kernels = jnp.stack([kernel_f, kernel_f[:, ::-1]])
    padded = jnp.pad(widened, ((0, 0), (3, 3), (0, 0), (0, 0)))
    conv = jnp.zeros((2, row_count, col_count, channels), jnp.float32)
    for row_off in range(7):
        for col_off in range(7):
            weights_here = kernels[:, row_off, col_off][:, None, None, :]
            conv = (
                conv
                + weights_here
                * padded[:, row_off : row_off + row_count, col_off : col_off + col_count]
            )
    mean_val = jnp.mean(conv, axis=-1, keepdims=True)
    centred = conv - mean_val
    variance = jnp.mean(centred * centred, axis=-1, keepdims=True)
    inverse = lax.rsqrt(variance + 1e-06)
    nhat = centred * inverse
    normed = (nhat * norm_gain).astype(jnp.bfloat16).reshape(-1, channels)
    pre = jnp.dot(normed, expand_weight, preferred_element_type=jnp.float32)
    activated, gelu_slope = gelu_parts(pre)
    hidden = rounded_f32(activated).astype(jnp.bfloat16)
    hiddens = hidden.astype(jnp.float32).reshape(2, pixels, hidden_size)
    contrast = (hiddens[0] - hiddens[1]).astype(jnp.bfloat16)
    contrast_t = contrast.T.reshape(outer, 2, 2, hidden_size // count, pixels)
    other_core = lambda i: i ^ 1
    other_side = lambda i: i ^ 2
    mates = [(0, 0), (0, 1), (1, 0), (1, 1)]
    contrast_parts = []
    for side_step, core_step in mates:
        part = pick(
            pick(contrast_t, lax.rem(core + core_step, 2), 2), lax.rem(side + side_step, 2), 1
        )
        hop = 2 * side_step + core_step
        contrast_parts.append(permuted(part, lambda i: i ^ hop) if hop else part)
    branch = jnp.dot(hidden, reduce_weight, preferred_element_type=jnp.float32)
    branch, contrast_parts = lax.optimization_barrier((branch, contrast_parts))
    outputs = rounded_f32(views + layer_scale * branch.reshape(conv.shape))
    difference = outputs[0] - outputs[1]
    disagreement = difference.astype(jnp.bfloat16)
    residual = (difference * (1.0 / math.sqrt(row_count * total_cols))).astype(jnp.bfloat16)
    residual = lax.optimization_barrier(residual)
    flat_grad = residual.astype(jnp.float32).reshape(pixels, channels)
    branches = branch.reshape(2, pixels, channels)
    grad_scale_local = jnp.sum((branches[0] - branches[1]) * flat_grad, axis=0)
    dbranch = (layer_scale * flat_grad).astype(jnp.bfloat16)

    dbranch_parts = [dbranch] + [permuted(dbranch, lambda i: i ^ hop) for hop in range(1, 4)]
    dhidden = lax.dot_general(
        dbranch, reduce_weight, (((1,), (1,)), ((), ())), preferred_element_type=jnp.float32
    )
    slopes = gelu_slope.reshape(2, pixels, hidden_size)
    dpre = jnp.stack([dhidden * slopes[0], -dhidden * slopes[1]]).astype(jnp.bfloat16)
    dpre = dpre.reshape(2 * pixels, hidden_size)

    dpre, dbranch_parts = lax.optimization_barrier((dpre, dbranch_parts))
    contrast_quad = jnp.concatenate(contrast_parts, axis=-1)
    dbranch_quad = jnp.concatenate(dbranch_parts, axis=0)
    reduce_quad = jnp.dot(
        contrast_quad.reshape(-1, 4 * pixels), dbranch_quad, preferred_element_type=jnp.float32
    ).reshape(outer, hidden_size // count, channels)
    normed_t = normed.T.reshape(outer, 2, 2, channels // count, 2 * pixels)
    normed_pair = jnp.concatenate(
        [pick(normed_t, core, 2), permuted(pick(normed_t, 1 - core, 2), other_core)], axis=-1
    )
    dpre_pair = jnp.concatenate([dpre, permuted(dpre, other_core)], axis=0)

    def expand_part(which):
        rows = pick(normed_pair, which, 1).reshape(-1, 4 * pixels)
        return jnp.dot(rows, dpre_pair, preferred_element_type=jnp.float32)

    leaving = expand_part(1 - side).astype(jnp.bfloat16)
    arrived = permuted(leaving, other_side)
    reduce_rounded = reduce_quad.astype(jnp.bfloat16)
    reduce_arrived = outer_exchange(reduce_rounded)
    small = tail(
        after(dpre, leaving, reduce_rounded),
        expand_weight,
        nhat,
        inverse,
        norm_gain,
        grad_scale_local,
        widened,
    )
    small, reduce_arrived = lax.optimization_barrier((small, reduce_arrived))
    halves = small.reshape(2, -1, channels)
    half = pick(halves, core, 0) + permuted(pick(halves, 1 - core, 0), other_core)
    for bit in range(2, count.bit_length() - 1):
        half = half + permuted(half, lambda i: i ^ (1 << bit))
    arrived, half = lax.optimization_barrier((arrived, half))
    expand_quad = expand_part(side) + arrived.astype(jnp.float32)
    expand_quad = expand_quad.reshape(outer, channels // count, hidden_size)
    expand_arrived = outer_exchange(expand_quad.astype(jnp.bfloat16))
    grad_reduce = outer_total(reduce_quad, reduce_arrived)
    half = half + permuted(half, other_side)
    other_half = permuted(half, other_core)
    small = jnp.concatenate(
        [jnp.where(core == 0, half, other_half), jnp.where(core == 0, other_half, half)], axis=0
    )
    grad_expand = outer_total(expand_quad, expand_arrived)
    return (
        disagreement,
        grad_expand,
        grad_reduce,
        small[:49].reshape(7, 7, channels),
        small[49],
        small[50],
    )


def solution(mesh):
    in_specs = (P("groups", "col", None), P("col", None), P(), P(), P(), P(), P())
    out_specs = (
        P("groups", "col", None),
        P(("groups", "col"), None),
        P(("groups", "col"), None),
        P("groups", None, None),
        P("groups"),
        P("groups"),
    )
    return jax.shard_map(
        on_device, mesh=mesh, in_specs=in_specs, out_specs=out_specs, check_vma=False
    )
```

```python
import math

import jax
import jax.numpy as jnp
from jax import lax
from jax.experimental import pallas as pl
from jax.experimental.pallas import tpu as pltpu
from jax.sharding import PartitionSpec as P


def permuted(block, target):
    count = lax.axis_size("col")
    return lax.ppermute(block, "col", [(i, target(i)) for i in range(count)])


def gelu_parts(pre):
    normal_cdf = 0.5 * (1.0 + jax.scipy.special.erf(pre * 0.7071067811865476))
    density = jnp.exp(-0.5 * pre * pre) * 0.3989422804014327
    return (pre * normal_cdf, normal_cdf + pre * density)


def rounded_f32(value):
    return lax.reduce_precision(value, 8, 7)


def with_halo(block, width):
    count = lax.axis_size("col")
    forward = [(i, i + 1) for i in range(count - 1)]
    backward = [(target, source) for source, target in forward]
    low = lax.ppermute(block[:, :, -width:], "col", forward)
    high = lax.ppermute(block[:, :, :width], "col", backward)
    return jnp.concatenate([low, block, high], axis=2)


def pick(array, index, axis):
    return lax.dynamic_index_in_dim(array, index, axis, keepdims=False)


def outer_exchange(rounded):
    outer = rounded.shape[0]
    count = lax.axis_size("col")
    mine = lax.axis_index("col") // 4
    return [
        permuted(pick(rounded, lax.rem(mine + step, outer), 0), lambda i: (i + 4 * step) % count)
        for step in range(1, outer)
    ]


def outer_total(partial, arrived):
    total = pick(partial, lax.axis_index("col") // 4, 0)
    for block in arrived:
        total = total + block.astype(jnp.float32)
    return total


def tail_kernel(
    dpre_ref, weight_ref, nhat_ref, inverse_ref, gain_ref, scale_ref, views_ref, out_ref, dconv_ref
):
    _, rows, wide, channels = views_ref.shape
    cols = wide - 6
    dnormed = lax.dot_general(
        dpre_ref[...],
        weight_ref[...],
        (((1,), (1,)), ((), ())),
        preferred_element_type=jnp.float32,
    )
    nhat = nhat_ref[...]
    out_ref[49:50] = jnp.sum(dnormed * nhat, axis=0, keepdims=True)
    out_ref[50:51] = scale_ref[...]
    out_ref[51:64] = jnp.zeros((13, channels), jnp.float32)
    scaled = dnormed * gain_ref[...]
    dconv = inverse_ref[...] * (
        scaled
        - jnp.mean(scaled, axis=-1, keepdims=True)
        - nhat * jnp.mean(scaled * nhat, axis=-1, keepdims=True)
    )
    dconv_ref[...] = dconv.reshape(dconv_ref.shape)

    def channel_tile(tile, carry):
        lanes = pl.ds(pl.multiple_of(tile * 128, 128), 128)
        sums = [[jnp.zeros((cols, 128), jnp.float32) for _ in range(7)] for _ in range(7)]
        for view in range(2):
            grads = [dconv_ref[view, row, :, lanes] for row in range(rows)]
            for source in range(rows):
                for col_off in range(7):
                    window = views_ref[view, source, col_off : col_off + cols, lanes]
                    place = col_off if view == 0 else 6 - col_off
                    for row_off in range(7):
                        row = source - row_off + 3
                        if 0 <= row < rows:
                            sums[row_off][place] = sums[row_off][place] + window * grads[row]
        for row_off in range(7):
            for col_off in range(7):
                index = row_off * 7 + col_off
                out_ref[index : index + 1, lanes] = jnp.sum(
                    sums[row_off][col_off], axis=0, keepdims=True
                )
        return carry

    lax.fori_loop(0, channels // 128, channel_tile, 0)


def tail(dpre, expand_weight, nhat, inverse, norm_gain, grad_scale, widened):
    channels = nhat.shape[-1]
    view_count, rows, wide, _ = widened.shape
    return pl.pallas_call(
        tail_kernel,
        out_shape=jax.ShapeDtypeStruct((64, channels), jnp.float32),
        scratch_shapes=[pltpu.VMEM((view_count, rows, wide - 6, channels), jnp.float32)],
        compiler_params=pltpu.CompilerParams(vmem_limit_bytes=32 << 20),
        cost_estimate=pl.CostEstimate(
            flops=20_000_000_000, bytes_accessed=30_000_000, transcendentals=0
        ),
    )(
        dpre,
        expand_weight,
        nhat.reshape(-1, channels),
        inverse.reshape(-1, 1),
        norm_gain[None],
        grad_scale[None],
        widened.astype(jnp.float32),
    )


def after(value, *others):
    return lax.optimization_barrier((value, *others))[0]


def on_device(
    features, column_table, dw_kernel, norm_gain, expand_weight, reduce_weight, layer_scale
):
    row_count, col_count, channels = features.shape
    count = lax.axis_size("col")
    outer = count // 4
    me = lax.axis_index("col")
    core = lax.rem(me, 2)
    side = lax.rem(me // 2, 2)
    total_cols = col_count * count
    hidden_size = expand_weight.shape[1]
    pixels = row_count * col_count

    mirrored_table = permuted(column_table, lambda i: count - 1 - i)[::-1]
    tables = jnp.stack([column_table, mirrored_table]).astype(jnp.float32)
    view_values = rounded_f32(features.astype(jnp.float32)[None] + tables[:, None])
    views = view_values.astype(jnp.bfloat16)
    kernel_f = dw_kernel.astype(jnp.float32)
    widened = with_halo(views, 3)
    padded = jnp.pad(widened.astype(jnp.float32), ((0, 0), (3, 3), (0, 0), (0, 0)))
    conv = jnp.zeros((2, row_count, col_count, channels), jnp.float32)
    for row_off in range(7):
        for col_off in range(7):
            weights_here = jnp.stack([kernel_f[row_off, col_off], kernel_f[row_off, 6 - col_off]])
            weights_here = weights_here[:, None, None, :]
            conv = (
                conv
                + weights_here
                * padded[:, row_off : row_off + row_count, col_off : col_off + col_count]
            )
    mean_val = jnp.mean(conv, axis=-1, keepdims=True)
    centred = conv - mean_val
    variance = jnp.mean(centred * centred, axis=-1, keepdims=True)
    inverse = lax.rsqrt(variance + 1e-06)
    nhat = centred * inverse
    normed = (nhat * norm_gain).astype(jnp.bfloat16).reshape(-1, channels)
    pre = jnp.dot(normed, expand_weight, preferred_element_type=jnp.float32)
    activated, gelu_slope = gelu_parts(pre)
    hidden = rounded_f32(activated).astype(jnp.bfloat16)
    branch = jnp.dot(hidden, reduce_weight, preferred_element_type=jnp.float32)
    outputs = rounded_f32(view_values + layer_scale * branch.reshape(conv.shape))
    difference = outputs[0] - outputs[1]
    disagreement = difference.astype(jnp.bfloat16)
    residual = (difference * (1.0 / math.sqrt(row_count * total_cols))).astype(jnp.bfloat16)
    residual = lax.optimization_barrier(residual)
    flat_grad = residual.astype(jnp.float32).reshape(pixels, channels)
    branches = branch.reshape(2, pixels, channels)
    grad_scale_local = jnp.sum((branches[0] - branches[1]) * flat_grad, axis=0)
    dbranch = (layer_scale * flat_grad).astype(jnp.bfloat16)

    hiddens = hidden.astype(jnp.float32).reshape(2, pixels, hidden_size)
    contrast = (hiddens[0] - hiddens[1]).astype(jnp.bfloat16)
    contrast_t = contrast.T.reshape(outer, 2, 2, hidden_size // count, pixels)
    other_core = lambda i: i ^ 1
    other_side = lambda i: i ^ 2
    contrast_pair = jnp.concatenate(
        [pick(contrast_t, core, 2), permuted(pick(contrast_t, 1 - core, 2), other_core)], axis=-1
    )
    dbranch_pair = jnp.concatenate([dbranch, permuted(dbranch, other_core)], axis=0)
    contrast_near = pick(contrast_pair, side, 1)
    contrast_far = permuted(pick(contrast_pair, 1 - side, 1), other_side)
    dbranch_far = permuted(dbranch_pair, other_side)

    dhidden = lax.dot_general(
        dbranch, reduce_weight, (((1,), (1,)), ((), ())), preferred_element_type=jnp.float32
    )
    slopes = gelu_slope.reshape(2, pixels, hidden_size)
    dpre = jnp.stack([dhidden * slopes[0], -dhidden * slopes[1]]).astype(jnp.bfloat16)
    dpre = dpre.reshape(2 * pixels, hidden_size)

    normed_t = normed.T.reshape(outer, 2, 2, channels // count, 2 * pixels)
    normed_pair = jnp.concatenate(
        [pick(normed_t, core, 2), permuted(pick(normed_t, 1 - core, 2), other_core)], axis=-1
    )
    dpre_pair = jnp.concatenate([dpre, permuted(dpre, other_core)], axis=0)

    def expand_part(which):
        rows = pick(normed_pair, which, 1).reshape(-1, 4 * pixels)
        return jnp.dot(rows, dpre_pair, preferred_element_type=jnp.float32)

    leaving = expand_part(1 - side).astype(jnp.bfloat16)
    arrived = permuted(leaving, other_side)
    contrast_near, dbranch_pair, _ = lax.optimization_barrier(
        (contrast_near, dbranch_pair, leaving)
    )
    contrast_quad = jnp.concatenate([contrast_near, contrast_far], axis=-1)
    dbranch_quad = jnp.concatenate([dbranch_pair, dbranch_far], axis=0)
    reduce_quad = jnp.dot(
        contrast_quad.reshape(-1, 4 * pixels), dbranch_quad, preferred_element_type=jnp.float32
    ).reshape(outer, hidden_size // count, channels)
    reduce_rounded = reduce_quad.astype(jnp.bfloat16)
    reduce_arrived = outer_exchange(reduce_rounded)
    small = tail(
        after(dpre, leaving, reduce_rounded),
        expand_weight,
        nhat,
        inverse,
        norm_gain,
        grad_scale_local,
        widened,
    )
    small, reduce_arrived[0] = lax.optimization_barrier((small, reduce_arrived[0]))
    halves = small.reshape(2, -1, channels)
    half = pick(halves, core, 0) + permuted(pick(halves, 1 - core, 0), other_core)
    half_rounded = half.astype(jnp.bfloat16)
    half_arrived = [
        permuted(half_rounded, lambda i: (i + 4 * step) % count) for step in range(1, outer)
    ]
    arrived, half_arrived = lax.optimization_barrier((arrived, half_arrived))
    expand_quad = expand_part(side) + arrived.astype(jnp.float32)
    expand_quad = expand_quad.reshape(outer, channels // count, hidden_size)
    expand_arrived = outer_exchange(expand_quad.astype(jnp.bfloat16))
    grad_reduce = outer_total(reduce_quad, reduce_arrived)
    for block in half_arrived:
        half = half + block.astype(jnp.float32)
    half = half + permuted(half, other_side)
    other_half = permuted(half, other_core)
    small = jnp.concatenate(
        [jnp.where(core == 0, half, other_half), jnp.where(core == 0, other_half, half)], axis=0
    )
    grad_expand = outer_total(expand_quad, expand_arrived)
    return (
        disagreement,
        grad_expand,
        grad_reduce,
        small[:49].reshape(7, 7, channels),
        small[49],
        small[50],
    )


def solution(mesh):
    in_specs = (P("groups", "col", None), P("col", None), P(), P(), P(), P(), P())
    out_specs = (
        P("groups", "col", None),
        P(("groups", "col"), None),
        P(("groups", "col"), None),
        P("groups", None, None),
        P("groups"),
        P("groups"),
    )
    return jax.shard_map(
        on_device, mesh=mesh, in_specs=in_specs, out_specs=out_specs, check_vma=False
    )
```
